256 devices in a mesh: row: 16 (over y_hi, z), col: 16 (over x, y_lo, core).
Axes of the slice: x: 4, y: 4 (y_hi: 2, y_lo: 2; y = y_hi * 2 + y_lo), z: 8, core: 2. Of those that a mesh axis runs over, the one named last changes fastest.
Arguments:
- lesser: bfloat16 [16384, 16384], P('row', 'col'), may hold values from -6 to 6
- greater: bfloat16 [16384, 16384], P('row', 'col'), may hold values from -6 to 6
- screened_lesser: bfloat16 [16384, 16384], P('row', 'col'), may hold values from -6 to 6
- screened_greater: bfloat16 [16384, 16384], P('row', 'col'), may hold values from -6 to 6
Outputs:
- collision: float32 [16384, 4096], P('row', 'col')
The draws below stay inside these ranges and needn't reach their ends.
All inputs are finite; a program needn't handle non-finite values.
Results may differ from the reference program's by a relative error of at most 0.0051.
Values may be sent and summed in bfloat16 or wider, within the bound.
A program may use at most 64 MiB of HBM per device.

```python
import jax
import jax.numpy as jnp
from jax import lax

TILE_ORDER = 1024
WINDOW = 256
SLAB_ORDER = 16384
ROWS_DEV = 1024
N_ROW = 16
N_COL = 16


def levels(rng, dims, pieces, low, largest):
    level = 1.0
    for position, blocks in pieces:
        draws = jax.random.uniform(jax.random.fold_in(jax.random.fold_in(rng, 6), position), (blocks,), jnp.float32, low / len(pieces), largest / len(pieces))
        level = level * jnp.repeat(jnp.exp(draws), dims[position] // blocks).reshape((-1,) + (1,) * (len(dims) - 1 - position))
    return level


def gaussian(stream_key, dims, scale, limit, split=(), held_as=jnp.bfloat16):
    level = levels(stream_key, dims, split, -0.22, 0.18) if split else 1.0
    values = jax.random.normal(stream_key, dims, jnp.float32) * scale * level
    return jnp.minimum(jnp.maximum(values, -limit), limit).astype(held_as)


def setup_inputs(seed: int = 0) -> dict:
    streams_of = jax.random.split(jax.random.key(seed), 5)
    lesser = gaussian(streams_of[0], (SLAB_ORDER, SLAB_ORDER), 1.0, 6.0, ((0, 16), (1, 16)))
    greater = gaussian(streams_of[1], (SLAB_ORDER, SLAB_ORDER), 1.0, 6.0, ((0, 16), (1, 16)))
    screened_lesser = gaussian(streams_of[2], (SLAB_ORDER, SLAB_ORDER), 1.0, 6.0, ((0, 16), (1, 16)))
    screened_greater = gaussian(streams_of[3], (SLAB_ORDER, SLAB_ORDER), 1.0, 6.0, ((0, 16), (1, 16)))
    return {"lesser": lesser, "greater": greater, "screened_lesser": screened_lesser, "screened_greater": screened_greater}


def reference(lesser, greater, screened_lesser, screened_greater):
    slab = lesser.shape[0]
    scale = float(slab) ** -0.5

    def one_block(block):
        start = (block * ROWS_DEV).astype(jnp.int32)
        zero = jnp.zeros((), jnp.int32)
        less_rows = lax.dynamic_slice(lesser, (start, zero), (ROWS_DEV, slab)).astype(jnp.float32)
        great_rows = lax.dynamic_slice(greater, (start, zero), (ROWS_DEV, slab)).astype(jnp.float32)
        wless_rows = lax.dynamic_slice(screened_lesser, (start, zero), (ROWS_DEV, slab)).astype(jnp.float32)
        wgreat_rows = lax.dynamic_slice(screened_greater, (start, zero), (ROWS_DEV, slab)).astype(jnp.float32)
        prod_less = less_rows * wless_rows
        prod_great = great_rows * wgreat_rows
        sigma_less = prod_less.astype(jnp.bfloat16)
        later = start + jnp.arange(ROWS_DEV, dtype=jnp.int32)
        inner = jnp.arange(slab, dtype=jnp.int32)
        sigma_ret = jnp.where(inner[None, :] <= later[:, None], prod_great - prod_less, 0.0).astype(jnp.bfloat16)
        green_win = lax.dynamic_slice(lesser, (zero, start), (slab, WINDOW))
        great_win = lax.dynamic_slice(greater, (zero, start), (slab, WINDOW))
        diff_win = (green_win.astype(jnp.float32) - great_win.astype(jnp.float32)).astype(jnp.bfloat16)
        window_times = start + jnp.arange(WINDOW, dtype=jnp.int32)
        diff_win = jnp.where(inner[:, None] <= window_times[None, :], diff_win, jnp.zeros((), jnp.bfloat16))
        ret_tiles = sigma_ret.reshape(ROWS_DEV, N_COL, TILE_ORDER).astype(jnp.float32)
        less_tiles = sigma_less.reshape(ROWS_DEV, N_COL, TILE_ORDER).astype(jnp.float32)
        green_tiles = green_win.reshape(N_COL, TILE_ORDER, WINDOW).astype(jnp.float32)
        diff_tiles = diff_win.reshape(N_COL, TILE_ORDER, WINDOW).astype(jnp.float32)
        partial_value = jnp.einsum("tcu,cuw->tcw", ret_tiles, green_tiles) + jnp.einsum("tcu,cuw->tcw", less_tiles, diff_tiles)
        partial_value = scale * partial_value
        return jnp.cumsum(partial_value, axis=1).reshape(ROWS_DEV, N_COL * WINDOW)

    blocks = lax.map(one_block, jnp.arange(N_ROW, dtype=jnp.int32))
    return blocks.reshape(N_ROW * ROWS_DEV, N_COL * WINDOW)
```

```python
import functools

import jax
import jax.numpy as jnp
from jax import lax
from jax.experimental import pallas as pl
from jax.experimental.pallas import tpu as pltpu
from jax.sharding import PartitionSpec as P

WINDOW = 256
TILE = 1024
N = 16
CHIPS = 8
SCALE = 2.0**-7
MESH = pl.DeviceIdType.MESH

PLAN = (
    ((0, 0), (0, 2), (0, 14), (1, 2)),
    ((0, 0), (0, 12), (1, 2), (1, 14)),
    ((0, 0), (0, 4), (0, 6), (0, 12)),
)
PIECES = len(PLAN[0])
PIECE = TILE // PIECES
HALF = TILE // 2
PART = HALF // CHIPS


def pick(cls, values):
    out = jnp.int32(values[2])
    out = jnp.where(cls == 1, jnp.int32(values[1]), out)
    return jnp.where(cls == 0, jnp.int32(values[0]), out)


def kernel(
    less_hbm, great_hbm, wless_hbm, wgreat_hbm, out_ref,
    less, great, wless, wgreat, ret_s, less_s, win, slots, acc,
    pal, qsend, qrecv, esend, erecv, ysend, yrecv,
    load_sem, s1_send, s1_recv, f_send, win_recv,
    pal_send, pal_recv, q_send, q_recv, e_send, e_recv, y_send, y_recv,
):
    row = lax.axis_index("row")
    col = lax.axis_index("col")
    is_source = row < col
    is_lower = row > col
    works = row >= col
    core = col % 2
    chip = col // 2

    def at(r, c):
        return (r, c)

    barrier = pltpu.get_barrier_semaphore()

    def greet(r, c):
        pl.semaphore_signal(barrier, inc=1, device_id=at(r, c), device_id_type=MESH)

    relays = []
    count = jnp.int32(CHIPS)
    for j in range(1, PIECES):
        for cls in range(3):
            flip, mask = PLAN[cls][j]
            k = row ^ (8 * flip)
            r = col ^ mask
            a, b = ((0, 0), (0, 1), (1, 1))[cls]
            valid = (k < r) & (k // 8 == a) & (r // 8 == b)
            relays.append((cls, j, valid, k, r))
            count = count + valid.astype(jnp.int32)

            @pl.when(valid)
            def _():
                greet(k, r)

    cls_to = col // 8 + row // 8
    cls_from = row // 8 + col // 8
    count = count + jnp.where(is_source, PIECES, 0).astype(jnp.int32)

    @pl.when(is_lower)
    def _():
        for j in range(PIECES):
            f = pick(cls_to, [PLAN[c][j][0] for c in range(3)])
            m = pick(cls_to, [PLAN[c][j][1] for c in range(3)])
            greet(col ^ (8 * f), row ^ m)

    greet(row, col ^ 1)
    for d in range(1, CHIPS):
        greet(row, ((chip + d) % CHIPS) * 2 + core)

    STEPS = 4
    SR = TILE // STEPS

    def loads(i):
        rows = pl.ds(i * SR, SR)
        return [
            pltpu.make_async_copy(h.at[rows], v.at[rows], load_sem.at[i, n])
            for n, (h, v) in enumerate(
                ((less_hbm, less), (great_hbm, great), (wless_hbm, wless), (wgreat_hbm, wgreat))
            )
        ]

    def own_windows():
        out = []
        for j in range(PIECES):
            rows = pl.ds(j * PIECE, PIECE)
            for n, h in enumerate((less_hbm, great_hbm)):
                out.append(
                    pltpu.make_async_copy(
                        h.at[rows, pl.ds(0, WINDOW)], win.at[j, n], win_recv.at[j]
                    )
                )
        return out

    @pl.when(works)
    def _():
        for i in range(STEPS):
            for cp in loads(i):
                cp.start()

        @pl.when(row == col)
        def _():
            for cp in own_windows():
                cp.start()

        B = 16
        for i in range(STEPS):
            for cp in loads(i):
                cp.wait()

            @pl.loop(0, SR // B)
            def _(s):
                base = i * SR + s * B
                rows = pl.ds(pl.multiple_of(base, B), B)
                low = less[rows, :].astype(jnp.float32) * wless[rows, :].astype(jnp.float32)
                high = great[rows, :].astype(jnp.float32) * wgreat[rows, :].astype(jnp.float32)
                less_s[rows, :] = low.astype(jnp.bfloat16)
                later = row * TILE + base + lax.broadcasted_iota(jnp.int32, (B, TILE), 0)
                inner = col * TILE + lax.broadcasted_iota(jnp.int32, (B, TILE), 1)
                ret_s[rows, :] = jnp.where(inner <= later, high - low, 0.0).astype(jnp.bfloat16)

    pl.semaphore_wait(barrier, count)

    def first_sends(j, part):
        f = pick(cls_from, [PLAN[c][j][0] for c in range(3)])
        m = pick(cls_from, [PLAN[c][j][1] for c in range(3)])
        h = (less_hbm, great_hbm)[part]
        src = h.at[pl.ds(j * PIECE, PIECE), pl.ds(0, WINDOW)]
        if j == 0:
            return pltpu.make_async_remote_copy(
                src, win.at[0, part], s1_send.at[j, part], win_recv.at[0],
                device_id=at(col, row), device_id_type=MESH,
            )
        slot = (j - 1) * 3 + cls_from
        return pltpu.make_async_remote_copy(
            src, slots.at[slot, part], s1_send.at[j, part], s1_recv.at[slot],
            device_id=at(row ^ (8 * f), col ^ m), device_id_type=MESH,
        )

    @pl.when(is_source)
    def _():
        for j in range(PIECES):
            for part in range(2):
                first_sends(j, part).start()

    def forward(i):
        cls, j, valid, k, r = relays[i]
        return pltpu.make_async_remote_copy(
            slots.at[i], win.at[j], f_send.at[i], win_recv.at[j],
            device_id=at(r, k), device_id_type=MESH,
        )

    for i, (cls, j, valid, k, r) in enumerate(relays):
        @pl.when(valid)
        def _():
            pltpu.make_async_copy(slots.at[i], slots.at[i], s1_recv.at[i]).wait()
            forward(i).start()

    MB = 256

    @pl.when(works)
    def _():
        for j in range(PIECES):
            pltpu.make_async_copy(win.at[j], win.at[j], win_recv.at[j]).wait()
            green = win[j, 0]
            diff = (green.astype(jnp.float32) - win[j, 1].astype(jnp.float32)).astype(jnp.bfloat16)
            inner = col * TILE + j * PIECE + lax.broadcasted_iota(jnp.int32, (PIECE, WINDOW), 0)
            times = row * TILE + lax.broadcasted_iota(jnp.int32, (PIECE, WINDOW), 1)
            diff = jnp.where(inner <= times, diff, jnp.zeros((), jnp.bfloat16))
            us = pl.ds(j * PIECE, PIECE)

            @pl.loop(0, TILE // MB)
            def _(s):
                rows = pl.ds(pl.multiple_of(s * MB, MB), MB)
                value = jnp.dot(ret_s[rows, us], green, preferred_element_type=jnp.float32)
                value = value + jnp.dot(less_s[rows, us], diff, preferred_element_type=jnp.float32)
                value = value * SCALE
                if j == 0:
                    acc[rows, :] = value
                else:
                    acc[rows, :] = acc[rows, :] + value

    @pl.when(is_source)
    def _():
        acc[...] = jnp.zeros_like(acc)

    mine = pl.ds(pl.multiple_of(core * HALF, HALF), HALF)
    other = pl.ds(pl.multiple_of((1 - core) * HALF, HALF), HALF)
    pal_id = at(row, col ^ 1)
    pal_copy = pltpu.make_async_remote_copy(
        acc.at[other], pal, pal_send, pal_recv, device_id=pal_id, device_id_type=MESH
    )
    pal_copy.start()
    pal_copy.wait_recv()
    both = acc[mine, :] + pal[...]
    qsend[...] = both.astype(jnp.bfloat16).reshape(CHIPS, PART, WINDOW)

    def q_copy(d):
        to = (chip + d) % CHIPS
        return pltpu.make_async_remote_copy(
            qsend.at[to], qrecv.at[chip], q_send.at[d], q_recv.at[chip],
            device_id=at(row, to * 2 + core), device_id_type=MESH,
        )

    for d in range(1, CHIPS):
        q_copy(d).start()
    qrecv[chip] = qsend[chip]
    for d in range(1, CHIPS):
        src = (chip + CHIPS - d) % CHIPS
        pltpu.make_async_copy(qrecv.at[src], qrecv.at[src], q_recv.at[src]).wait()
    run = jnp.zeros((PART, WINDOW), jnp.float32)
    for m in range(CHIPS):
        esend[m] = run.astype(jnp.bfloat16)
        run = run + qrecv[m].astype(jnp.float32)

    def e_copy(d):
        to = (chip + d) % CHIPS
        return pltpu.make_async_remote_copy(
            esend.at[to], erecv.at[chip], e_send.at[d], e_recv.at[chip],
            device_id=at(row, to * 2 + core), device_id_type=MESH,
        )

    for d in range(1, CHIPS):
        e_copy(d).start()
    erecv[chip] = esend[chip]
    for d in range(1, CHIPS):
        src = (chip + CHIPS - d) % CHIPS
        pltpu.make_async_copy(erecv.at[src], erecv.at[src], e_recv.at[src]).wait()
    earlier = erecv[...].astype(jnp.float32).reshape(HALF, WINDOW)
    own = acc[mine, :]
    first = core == 0
    ysend[...] = earlier + jnp.where(first, own, 0.0)
    y_copy = pltpu.make_async_remote_copy(
        ysend, yrecv, y_send, y_recv, device_id=pal_id, device_id_type=MESH
    )
    y_copy.start()
    out_ref[mine, :] = earlier + own + jnp.where(first, 0.0, pal[...])
    y_copy.wait_recv()
    out_ref[other, :] = yrecv[...] + acc[other, :]

    @pl.when(is_source)
    def _():
        for j in range(PIECES):
            for part in range(2):
                first_sends(j, part).wait_send()

    for i, (cls, j, valid, k, r) in enumerate(relays):
        @pl.when(valid)
        def _():
            forward(i).wait_send()

    pal_copy.wait_send()
    y_copy.wait_send()
    for d in range(1, CHIPS):
        q_copy(d).wait_send()
        e_copy(d).wait_send()


def local(lesser, greater, screened_lesser, screened_greater):
    bf16, f32 = jnp.bfloat16, jnp.float32
    n_slots = 3 * (PIECES - 1)
    dma = pltpu.SemaphoreType.DMA
    return pl.pallas_call(
        kernel,
        out_shape=jax.ShapeDtypeStruct((TILE, WINDOW), f32),
        in_specs=[pl.BlockSpec(memory_space=pl.ANY)] * 4,
        out_specs=pl.BlockSpec(memory_space=pltpu.VMEM),
        scratch_shapes=[pltpu.VMEM((TILE, TILE), bf16)] * 6
        + [
            pltpu.VMEM((PIECES, 2, PIECE, WINDOW), bf16),
            pltpu.VMEM((n_slots, 2, PIECE, WINDOW), bf16),
            pltpu.VMEM((TILE, WINDOW), f32),
            pltpu.VMEM((HALF, WINDOW), f32),
            pltpu.VMEM((CHIPS, PART, WINDOW), bf16),
            pltpu.VMEM((CHIPS, PART, WINDOW), bf16),
            pltpu.VMEM((CHIPS, PART, WINDOW), bf16),
            pltpu.VMEM((CHIPS, PART, WINDOW), bf16),
            pltpu.VMEM((HALF, WINDOW), f32),
            pltpu.VMEM((HALF, WINDOW), f32),
            dma((4, 4)),
            dma((PIECES, 2)),
            dma((n_slots,)),
            dma((n_slots,)),
            dma((PIECES,)),
            dma(()),
            dma(()),
            dma((CHIPS,)),
            dma((CHIPS,)),
            dma((CHIPS,)),
            dma((CHIPS,)),
            dma(()),
            dma(()),
        ],
        compiler_params=pltpu.CompilerParams(
            collective_id=0, has_side_effects=True, vmem_limit_bytes=48 << 20
        ),
        name="collision",
    )(lesser, greater, screened_lesser, screened_greater)


def solution(mesh):
    spec = P("row", "col")
    return jax.shard_map(
        local, mesh=mesh, in_specs=(spec,) * 4, out_specs=spec, check_vma=False
    )
```

```python
import functools

import jax
import jax.numpy as jnp
from jax import lax
from jax.experimental import pallas as pl
from jax.experimental.pallas import tpu as pltpu
from jax.sharding import PartitionSpec as P

WINDOW = 256
TILE = 1024
N = 16
CHIPS = 8
SCALE = 2.0**-7
MESH = pl.DeviceIdType.MESH

PLAN = (((0, 0), (0, 2), (0, 4), (0, 6), (0, 14), (1, 0), (1, 2), (0, 3), (0, 5), (0, 7), (0, 15), (1, 3), (0, 2), (0, 4), (0, 6), (1, 2)), ((0, 0), (0, 2), (0, 4), (0, 6), (0, 8), (1, 0), (1, 2), (1, 4), (1, 6), (1, 14), (0, 9), (1, 1), (1, 3), (1, 7), (1, 15), (1, 14)), ((0, 0), (0, 2), (0, 4), (0, 6), (0, 8), (0, 12), (1, 0), (1, 2), (1, 4), (0, 5), (0, 9), (0, 13), (1, 1), (1, 3), (1, 5), (0, 12)))
PIECES = len(PLAN[0])
PIECE = TILE // PIECES
GROUPS = 4
GROUP = TILE // GROUPS
PER = PIECES // GROUPS
HALF = TILE // 2
PART = HALF // CHIPS


def pick(cls, values):
    out = jnp.int32(values[2])
    out = jnp.where(cls == 1, jnp.int32(values[1]), out)
    return jnp.where(cls == 0, jnp.int32(values[0]), out)


def kernel(
    less_hbm, great_hbm, wless_hbm, wgreat_hbm, out_ref,
    less, great, wless, wgreat, ret_s, less_s, win, slots, acc,
    pal, qsend, qrecv, esend, erecv, ysend, yrecv,
    near_sem, far_sem, load_sem, s1_send, s1_recv, f_send, win_recv,
    pal_send, pal_recv, q_send, q_recv, e_send, e_recv, y_send, y_recv,
):
    row = lax.axis_index("row")
    col = lax.axis_index("col")
    is_source = row < col
    is_lower = row > col
    works = row >= col
    core = col % 2
    chip = col // 2

    def at(r, c):
        return (r, c)

    barrier = pltpu.get_barrier_semaphore()

    def greet(r, c):
        pl.semaphore_signal(barrier, inc=1, device_id=at(r, c), device_id_type=MESH)

    relays = []
    for j in range(1, PIECES):
        for cls in range(3):
            flip, mask = PLAN[cls][j]
            k = row ^ (8 * flip)
            r = col ^ mask
            a, b = ((0, 0), (0, 1), (1, 1))[cls]
            valid = (k < r) & (k // 8 == a) & (r // 8 == b)
            relays.append((cls, j, valid, k, r))
    cls_from = row // 8 + col // 8

    for d in range(1, N):
        greet(row, (col + d) % N)
    for d in range(N):
        greet(row ^ 8, (col + d) % N)

    def along(d):
        return row // 8 * 8 + (row + d) % 8

    near = (1, 2, 6, 7)
    far = (3, 4, 5)
    for d in near:
        greet(along(d), col)

    STEPS = 4
    SR = TILE // STEPS

    def loads(i):
        rows = pl.ds(i * SR, SR)
        return [
            pltpu.make_async_copy(h.at[rows], v.at[rows], load_sem.at[i, n])
            for n, (h, v) in enumerate(
                ((less_hbm, less), (great_hbm, great), (wless_hbm, wless), (wgreat_hbm, wgreat))
            )
        ]

    def own_windows():
        out = []
        for j in range(PIECES):
            rows = pl.ds(j * PIECE, PIECE)
            for n, h in enumerate((less_hbm, great_hbm)):
                out.append(
                    pltpu.make_async_copy(
                        h.at[rows, pl.ds(0, WINDOW)], win.at[j, n], win_recv.at[j]
                    )
                )
        return out

    @pl.when(works)
    def _():
        for i in range(STEPS):
            for cp in loads(i):
                cp.start()

        @pl.when(row == col)
        def _():
            for cp in own_windows():
                cp.start()

    pl.semaphore_wait(barrier, 2 * N - 1 + len(near))

    def first_sends(j, part):
        f = pick(cls_from, [PLAN[c][j][0] for c in range(3)])
        m = pick(cls_from, [PLAN[c][j][1] for c in range(3)])
        h = (less_hbm, great_hbm)[part]
        src = h.at[pl.ds(j * PIECE, PIECE), pl.ds(0, WINDOW)]
        if j == 0:
            return pltpu.make_async_remote_copy(
                src, win.at[0, part], s1_send.at[j, part], win_recv.at[0],
                device_id=at(col, row), device_id_type=MESH,
            )
        slot = (j - 1) * 3 + cls_from
        return pltpu.make_async_remote_copy(
            src, slots.at[slot, part], s1_send.at[j, part], s1_recv.at[slot],
            device_id=at(row ^ (8 * f), col ^ m), device_id_type=MESH,
        )

    @pl.when(is_source)
    def _():
        for j in range(1, PIECES):
            for part in range(2):
                first_sends(j, part).start()

    def tell(sem, steps):
        for d in steps:
            pl.semaphore_signal(
                sem, inc=1, device_id=at(along(d), col), device_id_type=MESH
            )

    tell(near_sem, near)
    pl.semaphore_wait(near_sem, len(near))
    tell(far_sem, far)

    @pl.when(works)
    def _():
        B = 16
        for i in range(STEPS):
            for cp in loads(i):
                cp.wait()

            @pl.loop(0, SR // B)
            def _(s):
                base = i * SR + s * B
                rows = pl.ds(pl.multiple_of(base, B), B)
                low = less[rows, :].astype(jnp.float32) * wless[rows, :].astype(jnp.float32)
                high = great[rows, :].astype(jnp.float32) * wgreat[rows, :].astype(jnp.float32)
                less_s[rows, :] = low.astype(jnp.bfloat16)
                later = row * TILE + base + lax.broadcasted_iota(jnp.int32, (B, TILE), 0)
                inner = col * TILE + lax.broadcasted_iota(jnp.int32, (B, TILE), 1)
                ret_s[rows, :] = jnp.where(inner <= later, high - low, 0.0).astype(jnp.bfloat16)

    pl.semaphore_wait(far_sem, len(far))

    @pl.when(is_source)
    def _():
        for part in range(2):
            first_sends(0, part).start()

    def forward(i):
        cls, j, valid, k, r = relays[i]
        return pltpu.make_async_remote_copy(
            slots.at[i], win.at[j], f_send.at[i], win_recv.at[j],
            device_id=at(r, k), device_id_type=MESH,
        )

    for i, (cls, j, valid, k, r) in enumerate(relays):
        @pl.when(valid)
        def _():
            pltpu.make_async_copy(slots.at[i], slots.at[i], s1_recv.at[i]).wait()
            forward(i).start()

    MB = 256

    @pl.when(works)
    def _():
        for g in range(GROUPS):
            for j in range(g * PER, (g + 1) * PER):
                pltpu.make_async_copy(win.at[j], win.at[j], win_recv.at[j]).wait()
            pieces = pl.ds(g * PER, PER)
            green = win[pieces, 0].reshape(GROUP, WINDOW)
            great_win = win[pieces, 1].reshape(GROUP, WINDOW).astype(jnp.float32)
            diff = (green.astype(jnp.float32) - great_win).astype(jnp.bfloat16)
            inner = col * TILE + g * GROUP + lax.broadcasted_iota(jnp.int32, (GROUP, WINDOW), 0)
            times = row * TILE + lax.broadcasted_iota(jnp.int32, (GROUP, WINDOW), 1)
            diff = jnp.where(inner <= times, diff, jnp.zeros((), jnp.bfloat16))
            us = pl.ds(g * GROUP, GROUP)

            @pl.loop(0, TILE // MB)
            def _(s):
                rows = pl.ds(pl.multiple_of(s * MB, MB), MB)
                value = jnp.dot(ret_s[rows, us], green, preferred_element_type=jnp.float32)
                value = value + jnp.dot(less_s[rows, us], diff, preferred_element_type=jnp.float32)
                value = value * SCALE
                if g == 0:
                    acc[rows, :] = value
                else:
                    acc[rows, :] = acc[rows, :] + value

    @pl.when(is_source)
    def _():
        acc[...] = jnp.zeros_like(acc)

    mine = pl.ds(pl.multiple_of(core * HALF, HALF), HALF)
    other = pl.ds(pl.multiple_of((1 - core) * HALF, HALF), HALF)
    pal_id = at(row, col ^ 1)
    pal_copy = pltpu.make_async_remote_copy(
        acc.at[other], pal, pal_send, pal_recv, device_id=pal_id, device_id_type=MESH
    )
    pal_copy.start()
    pal_copy.wait_recv()
    both = acc[mine, :] + pal[...]
    qsend[...] = both.astype(jnp.bfloat16).reshape(CHIPS, PART, WINDOW)

    def q_copy(d):
        to = (chip + d) % CHIPS
        return pltpu.make_async_remote_copy(
            qsend.at[to], qrecv.at[chip], q_send.at[d], q_recv.at[chip],
            device_id=at(row, to * 2 + core), device_id_type=MESH,
        )

    for d in range(1, CHIPS):
        q_copy(d).start()
    qrecv[chip] = qsend[chip]
    for d in range(1, CHIPS):
        src = (chip + CHIPS - d) % CHIPS
        pltpu.make_async_copy(qrecv.at[src], qrecv.at[src], q_recv.at[src]).wait()
    run = jnp.zeros((PART, WINDOW), jnp.float32)
    for m in range(CHIPS):
        esend[m] = run.astype(jnp.bfloat16)
        run = run + qrecv[m].astype(jnp.float32)

    def e_copy(d):
        to = (chip + d) % CHIPS
        return pltpu.make_async_remote_copy(
            esend.at[to], erecv.at[chip], e_send.at[d], e_recv.at[chip],
            device_id=at(row, to * 2 + core), device_id_type=MESH,
        )

    for d in range(1, CHIPS):
        e_copy(d).start()
    erecv[chip] = esend[chip]
    for d in range(1, CHIPS):
        src = (chip + CHIPS - d) % CHIPS
        pltpu.make_async_copy(erecv.at[src], erecv.at[src], e_recv.at[src]).wait()
    earlier = erecv[...].astype(jnp.float32).reshape(HALF, WINDOW)
    own = acc[mine, :]
    first = core == 0
    ysend[...] = earlier + jnp.where(first, own, 0.0)
    y_copy = pltpu.make_async_remote_copy(
        ysend, yrecv, y_send, y_recv, device_id=pal_id, device_id_type=MESH
    )
    y_copy.start()
    out_ref[mine, :] = earlier + own + jnp.where(first, 0.0, pal[...])
    y_copy.wait_recv()
    out_ref[other, :] = yrecv[...] + acc[other, :]

    @pl.when(is_source)
    def _():
        for j in range(PIECES):
            for part in range(2):
                first_sends(j, part).wait_send()

    for i, (cls, j, valid, k, r) in enumerate(relays):
        @pl.when(valid)
        def _():
            forward(i).wait_send()

    pal_copy.wait_send()
    y_copy.wait_send()
    for d in range(1, CHIPS):
        q_copy(d).wait_send()
        e_copy(d).wait_send()


def local(lesser, greater, screened_lesser, screened_greater):
    bf16, f32 = jnp.bfloat16, jnp.float32
    n_slots = 3 * (PIECES - 1)
    dma = pltpu.SemaphoreType.DMA
    return pl.pallas_call(
        kernel,
        out_shape=jax.ShapeDtypeStruct((TILE, WINDOW), f32),
        in_specs=[pl.BlockSpec(memory_space=pl.ANY)] * 4,
        out_specs=pl.BlockSpec(memory_space=pltpu.VMEM),
        scratch_shapes=[pltpu.VMEM((TILE, TILE), bf16)] * 6
        + [
            pltpu.VMEM((PIECES, 2, PIECE, WINDOW), bf16),
            pltpu.VMEM((n_slots, 2, PIECE, WINDOW), bf16),
            pltpu.VMEM((TILE, WINDOW), f32),
            pltpu.VMEM((HALF, WINDOW), f32),
            pltpu.VMEM((CHIPS, PART, WINDOW), bf16),
            pltpu.VMEM((CHIPS, PART, WINDOW), bf16),
            pltpu.VMEM((CHIPS, PART, WINDOW), bf16),
            pltpu.VMEM((CHIPS, PART, WINDOW), bf16),
            pltpu.VMEM((HALF, WINDOW), f32),
            pltpu.VMEM((HALF, WINDOW), f32),
            pltpu.SemaphoreType.REGULAR,
            pltpu.SemaphoreType.REGULAR,
            dma((4, 4)),
            dma((PIECES, 2)),
            dma((n_slots,)),
            dma((n_slots,)),
            dma((PIECES,)),
            dma(()),
            dma(()),
            dma((CHIPS,)),
            dma((CHIPS,)),
            dma((CHIPS,)),
            dma((CHIPS,)),
            dma(()),
            dma(()),
        ],
        compiler_params=pltpu.CompilerParams(
            collective_id=0, has_side_effects=True, vmem_limit_bytes=63 << 20
        ),
        name="collision",
    )(lesser, greater, screened_lesser, screened_greater)


def solution(mesh):
    spec = P("row", "col")
    return jax.shard_map(
        local, mesh=mesh, in_specs=(spec,) * 4, out_specs=spec, check_vma=False
    )
```

```python
import functools

import jax
import jax.numpy as jnp
from jax import lax
from jax.experimental import pallas as pl
from jax.experimental.pallas import tpu as pltpu
from jax.sharding import PartitionSpec as P

WINDOW = 256
TILE = 1024
N = 16
CHIPS = 8
SCALE = 2.0**-7
MESH = pl.DeviceIdType.MESH

PLAN = (((0, 0), (0, 2), (0, 4), (0, 6), (0, 14), (1, 0), (1, 2), (0, 3), (0, 5), (0, 7), (0, 15), (1, 3), (0, 2), (0, 4), (0, 6), (1, 2)), ((0, 0), (0, 2), (0, 4), (0, 6), (0, 8), (1, 0), (1, 2), (1, 4), (1, 6), (1, 14), (0, 9), (1, 1), (1, 3), (1, 7), (1, 15), (1, 14)), ((0, 0), (0, 2), (0, 4), (0, 6), (0, 8), (0, 12), (1, 0), (1, 2), (1, 4), (0, 5), (0, 9), (0, 13), (1, 1), (1, 3), (1, 5), (0, 12)))
PIECES = len(PLAN[0])
PIECE = TILE // PIECES
GROUPS = 4
GROUP = TILE // GROUPS
PER = PIECES // GROUPS
HALF = TILE // 2
SUBS = 2
SUB = HALF // SUBS
PART = SUB // CHIPS


def pick(cls, values):
    out = jnp.int32(values[2])
    out = jnp.where(cls == 1, jnp.int32(values[1]), out)
    return jnp.where(cls == 0, jnp.int32(values[0]), out)


def kernel(
    less_hbm, great_hbm, wless_hbm, wgreat_hbm, out_ref,
    less, great, wless, wgreat, ret_s, less_s, win, slots, acc,
    psend, pal, qsend, qrecv, esend, erecv, ysend, yrecv,
    near_sem, far_sem, load_sem, s1_send, s1_recv, f_send, win_recv,
    pal_send, pal_recv, q_send, q_recv, e_send, e_recv, y_send, y_recv,
):
    row = lax.axis_index("row")
    col = lax.axis_index("col")
    is_source = row < col
    is_lower = row > col
    works = row >= col
    core = col % 2
    chip = col // 2

    def at(r, c):
        return (r, c)

    barrier = pltpu.get_barrier_semaphore()

    def greet(r, c):
        pl.semaphore_signal(barrier, inc=1, device_id=at(r, c), device_id_type=MESH)

    relays = []
    for j in range(1, PIECES):
        for cls in range(3):
            flip, mask = PLAN[cls][j]
            k = row ^ (8 * flip)
            r = col ^ mask
            a, b = ((0, 0), (0, 1), (1, 1))[cls]
            valid = (k < r) & (k // 8 == a) & (r // 8 == b)
            relays.append((cls, j, valid, k, r))
    cls_from = row // 8 + col // 8

    for d in range(1, N):
        greet(row, (col + d) % N)
    for d in range(N):
        greet(row ^ 8, (col + d) % N)

    def along(d):
        return row // 8 * 8 + (row + d) % 8

    near = (1, 2, 6, 7)
    far = (3, 4, 5)
    for d in near:
        greet(along(d), col)

    STEPS = 4
    SR = TILE // STEPS

    def loads(i):
        rows = pl.ds(i * SR, SR)
        return [
            pltpu.make_async_copy(h.at[rows], v.at[rows], load_sem.at[i, n])
            for n, (h, v) in enumerate(
                ((less_hbm, less), (great_hbm, great), (wless_hbm, wless), (wgreat_hbm, wgreat))
            )
        ]

    def own_windows():
        out = []
        for j in range(PIECES):
            rows = pl.ds(j * PIECE, PIECE)
            for n, h in enumerate((less_hbm, great_hbm)):
                out.append(
                    pltpu.make_async_copy(
                        h.at[rows, pl.ds(0, WINDOW)], win.at[j, n], win_recv.at[j]
                    )
                )
        return out

    @pl.when(works)
    def _():
        for i in range(STEPS):
            for cp in loads(i):
                cp.start()

        @pl.when(row == col)
        def _():
            for cp in own_windows():
                cp.start()

    pl.semaphore_wait(barrier, 2 * N - 1 + len(near))

    def first_sends(j, part):
        f = pick(cls_from, [PLAN[c][j][0] for c in range(3)])
        m = pick(cls_from, [PLAN[c][j][1] for c in range(3)])
        h = (less_hbm, great_hbm)[part]
        src = h.at[pl.ds(j * PIECE, PIECE), pl.ds(0, WINDOW)]
        if j == 0:
            return pltpu.make_async_remote_copy(
                src, win.at[0, part], s1_send.at[j, part], win_recv.at[0],
                device_id=at(col, row), device_id_type=MESH,
            )
        slot = (j - 1) * 3 + cls_from
        return pltpu.make_async_remote_copy(
            src, slots.at[slot, part], s1_send.at[j, part], s1_recv.at[slot],
            device_id=at(row ^ (8 * f), col ^ m), device_id_type=MESH,
        )

    @pl.when(is_source)
    def _():
        for j in range(1, PIECES):
            for part in range(2):
                first_sends(j, part).start()

    def tell(sem, steps):
        for d in steps:
            pl.semaphore_signal(
                sem, inc=1, device_id=at(along(d), col), device_id_type=MESH
            )

    tell(near_sem, near)
    pl.semaphore_wait(near_sem, len(near))
    tell(far_sem, far)

    @pl.when(works)
    def _():
        B = 16
        for i in range(STEPS):
            for cp in loads(i):
                cp.wait()

            @pl.loop(0, SR // B)
            def _(s):
                base = i * SR + s * B
                rows = pl.ds(pl.multiple_of(base, B), B)
                low = less[rows, :].astype(jnp.float32) * wless[rows, :].astype(jnp.float32)
                high = great[rows, :].astype(jnp.float32) * wgreat[rows, :].astype(jnp.float32)
                less_s[rows, :] = low.astype(jnp.bfloat16)
                later = row * TILE + base + lax.broadcasted_iota(jnp.int32, (B, TILE), 0)
                inner = col * TILE + lax.broadcasted_iota(jnp.int32, (B, TILE), 1)
                ret_s[rows, :] = jnp.where(inner <= later, high - low, 0.0).astype(jnp.bfloat16)

    pl.semaphore_wait(far_sem, len(far))

    @pl.when(is_source)
    def _():
        for part in range(2):
            first_sends(0, part).start()

    def forward(i):
        cls, j, valid, k, r = relays[i]
        return pltpu.make_async_remote_copy(
            slots.at[i], win.at[j], f_send.at[i], win_recv.at[j],
            device_id=at(r, k), device_id_type=MESH,
        )

    for i, (cls, j, valid, k, r) in enumerate(relays):
        @pl.when(valid)
        def _():
            pltpu.make_async_copy(slots.at[i], slots.at[i], s1_recv.at[i]).wait()
            forward(i).start()

    pal_id = at(row, col ^ 1)
    first = core == 0

    def pal_copy(t):
        return pltpu.make_async_remote_copy(
            psend.at[t], pal.at[t], pal_send.at[t], pal_recv.at[t],
            device_id=pal_id, device_id_type=MESH,
        )

    def q_copy(t, d):
        to = (chip + d) % CHIPS
        return pltpu.make_async_remote_copy(
            qsend.at[t, to], qrecv.at[t, chip], q_send.at[t, d], q_recv.at[t, chip],
            device_id=at(row, to * 2 + core), device_id_type=MESH,
        )

    def e_copy(t, to):
        return pltpu.make_async_remote_copy(
            esend.at[t, to], erecv.at[t, chip], e_send.at[t, to], e_recv.at[t, chip],
            device_id=at(row, to * 2 + core), device_id_type=MESH,
        )

    def y_copy(t):
        return pltpu.make_async_remote_copy(
            ysend.at[t], yrecv.at[t], y_send.at[t], y_recv.at[t],
            device_id=pal_id, device_id_type=MESH,
        )

    MB = 512

    @pl.when(works)
    def _():
        for g in range(GROUPS):
            for j in range(g * PER, (g + 1) * PER):
                pltpu.make_async_copy(win.at[j], win.at[j], win_recv.at[j]).wait()
            pieces = pl.ds(g * PER, PER)
            green = win[pieces, 0].reshape(GROUP, WINDOW)
            great_win = win[pieces, 1].reshape(GROUP, WINDOW).astype(jnp.float32)
            diff = (green.astype(jnp.float32) - great_win).astype(jnp.bfloat16)
            inner = col * TILE + g * GROUP + lax.broadcasted_iota(jnp.int32, (GROUP, WINDOW), 0)
            times = row * TILE + lax.broadcasted_iota(jnp.int32, (GROUP, WINDOW), 1)
            diff = jnp.where(inner <= times, diff, jnp.zeros((), jnp.bfloat16))
            us = pl.ds(g * GROUP, GROUP)

            @pl.loop(0, TILE // MB)
            def _(s):
                start = (s + core + 1) * MB % TILE
                rows = pl.ds(pl.multiple_of(start, MB), MB)
                value = jnp.dot(ret_s[rows, us], green, preferred_element_type=jnp.float32)
                value = value + jnp.dot(less_s[rows, us], diff, preferred_element_type=jnp.float32)
                value = value * SCALE
                if g > 0:
                    value = acc[rows, :] + value
                acc[rows, :] = value
                if g == GROUPS - 1:
                    @pl.when(s == 0)
                    def _():
                        psend[...] = value.astype(jnp.bfloat16).reshape(SUBS, SUB, WINDOW)
                        for t in range(SUBS):
                            pal_copy(t).start()

    @pl.when(is_source)
    def _():
        acc[...] = jnp.zeros_like(acc)
        psend[...] = jnp.zeros_like(psend)
        for t in range(SUBS):
            pal_copy(t).start()

    def sub_rows(half, t):
        return pl.ds(pl.multiple_of(half * HALF + t * SUB, SUB), SUB)

    last = CHIPS - 1

    for t in range(SUBS):
        pal_copy(t).wait_recv()
        both = acc[sub_rows(core, t), :] + pal[t].astype(jnp.float32)
        qsend[t] = both.astype(jnp.bfloat16).reshape(CHIPS, PART, WINDOW)

        @pl.when(chip != last)
        def _():
            for d in range(1, CHIPS):
                q_copy(t, d).start()

        qrecv[t, chip] = qsend[t, chip]

    for t in range(SUBS):
        run = jnp.zeros((PART, WINDOW), jnp.float32)
        for m in range(last):
            @pl.when(chip != m)
            def _():
                pltpu.make_async_copy(qrecv.at[t, m], qrecv.at[t, m], q_recv.at[t, m]).wait()

            run = run + qrecv[t, m].astype(jnp.float32)
            esend[t, m + 1] = run.astype(jnp.bfloat16)

            @pl.when(chip != m + 1)
            def _():
                e_copy(t, m + 1).start()

        esend[t, 0] = jnp.zeros((PART, WINDOW), jnp.bfloat16)
        erecv[t, chip] = esend[t, chip]

    for t in range(SUBS):
        @pl.when(chip == 0)
        def _():
            erecv[t] = jnp.zeros((CHIPS, PART, WINDOW), jnp.bfloat16)

        @pl.when(chip != 0)
        def _():
            for m in range(CHIPS):
                @pl.when(chip != m)
                def _():
                    pltpu.make_async_copy(erecv.at[t, m], erecv.at[t, m], e_recv.at[t, m]).wait()

        earlier = erecv[t].astype(jnp.float32).reshape(SUB, WINDOW)
        own = acc[sub_rows(core, t), :]
        ysend[t] = (earlier + jnp.where(first, own, 0.0)).astype(jnp.bfloat16)
        y_copy(t).start()
        before = jnp.where(first, 0.0, pal[t].astype(jnp.float32))
        out_ref[sub_rows(core, t), :] = earlier + before + own

    for t in range(SUBS):
        y_copy(t).wait_recv()
        rows = sub_rows(1 - core, t)
        out_ref[rows, :] = yrecv[t].astype(jnp.float32) + acc[rows, :]

    @pl.when(is_source)
    def _():
        for j in range(PIECES):
            for part in range(2):
                first_sends(j, part).wait_send()

    for i, (cls, j, valid, k, r) in enumerate(relays):
        @pl.when(valid)
        def _():
            forward(i).wait_send()

    for t in range(SUBS):
        pal_copy(t).wait_send()
        y_copy(t).wait_send()

        @pl.when(chip != last)
        def _():
            for d in range(1, CHIPS):
                q_copy(t, d).wait_send()

        for m in range(1, CHIPS):
            @pl.when(chip != m)
            def _():
                e_copy(t, m).wait_send()


def local(lesser, greater, screened_lesser, screened_greater):
    bf16, f32 = jnp.bfloat16, jnp.float32
    n_slots = 3 * (PIECES - 1)
    dma = pltpu.SemaphoreType.DMA
    return pl.pallas_call(
        kernel,
        out_shape=jax.ShapeDtypeStruct((TILE, WINDOW), f32),
        in_specs=[pl.BlockSpec(memory_space=pl.ANY)] * 4,
        out_specs=pl.BlockSpec(memory_space=pltpu.VMEM),
        scratch_shapes=[pltpu.VMEM((TILE, TILE), bf16)] * 6
        + [
            pltpu.VMEM((PIECES, 2, PIECE, WINDOW), bf16),
            pltpu.VMEM((n_slots, 2, PIECE, WINDOW), bf16),
            pltpu.VMEM((TILE, WINDOW), f32),
            pltpu.VMEM((SUBS, SUB, WINDOW), bf16),
            pltpu.VMEM((SUBS, SUB, WINDOW), bf16),
            pltpu.VMEM((SUBS, CHIPS, PART, WINDOW), bf16),
            pltpu.VMEM((SUBS, CHIPS, PART, WINDOW), bf16),
            pltpu.VMEM((SUBS, CHIPS, PART, WINDOW), bf16),
            pltpu.VMEM((SUBS, CHIPS, PART, WINDOW), bf16),
            pltpu.VMEM((SUBS, SUB, WINDOW), bf16),
            pltpu.VMEM((SUBS, SUB, WINDOW), bf16),
            pltpu.SemaphoreType.REGULAR,
            pltpu.SemaphoreType.REGULAR,
            dma((4, 4)),
            dma((PIECES, 2)),
            dma((n_slots,)),
            dma((n_slots,)),
            dma((PIECES,)),
            dma((SUBS,)),
            dma((SUBS,)),
            dma((SUBS, CHIPS)),
            dma((SUBS, CHIPS)),
            dma((SUBS, CHIPS)),
            dma((SUBS, CHIPS)),
            dma((SUBS,)),
            dma((SUBS,)),
        ],
        compiler_params=pltpu.CompilerParams(
            collective_id=0, has_side_effects=True, vmem_limit_bytes=63 << 20
        ),
        name="collision",
    )(lesser, greater, screened_lesser, screened_greater)


def solution(mesh):
    spec = P("row", "col")
    return jax.shard_map(
        local, mesh=mesh, in_specs=(spec,) * 4, out_specs=spec, check_vma=False
    )
```

```python
import functools

import jax
import jax.numpy as jnp
from jax import lax
from jax.experimental import pallas as pl
from jax.experimental.pallas import tpu as pltpu
from jax.sharding import PartitionSpec as P

WINDOW = 256
TILE = 1024
N = 16
CHIPS = 8
SCALE = 2.0**-7
MESH = pl.DeviceIdType.MESH

PLAN = (
    (
        (0, 0), (0, 2), (0, 4), (0, 6), (1, 2), (0, 14), (0, 3), (0, 5),
        (0, 7), (1, 0), (1, 3), (0, 15), (0, 2), (0, 4), (0, 6), (1, 2),
    ),
    (
        (0, 0), (1, 6), (1, 14), (0, 2), (0, 8), (1, 0), (0, 4), (1, 2),
        (1, 4), (1, 7), (1, 15), (0, 3), (0, 9), (1, 1), (1, 6), (1, 14),
    ),
    (
        (0, 0), (0, 12), (0, 2), (0, 4), (0, 8), (1, 0), (1, 4), (0, 13),
        (1, 2), (1, 6), (0, 3), (0, 5), (0, 9), (1, 1), (1, 5), (0, 12),
    ),
)
PIECES = len(PLAN[0])
DIRECT = sum(way == (0, 0) for way in PLAN[0])
PIECE = TILE // PIECES
GROUPS = 4
GROUP = TILE // GROUPS
PER = PIECES // GROUPS
HALF = TILE // 2
SUBS = 2
SUB = HALF // SUBS
PART = SUB // CHIPS


def pick(cls, values):
    out = jnp.int32(values[2])
    out = jnp.where(cls == 1, jnp.int32(values[1]), out)
    return jnp.where(cls == 0, jnp.int32(values[0]), out)


def kernel(
    less_hbm, great_hbm, wless_hbm, wgreat_hbm, out_ref,
    less, great, wless, wgreat, ret_s, less_s, win, slots, acc,
    psend, pal, qsend, qrecv, esend, erecv, ysend, yrecv,
    near_sem, far_sem, load_sem, s1_send, s1_recv, f_send, win_recv,
    pal_send, pal_recv, q_send, q_recv, e_send, e_recv, y_send, y_recv,
):
    row = lax.axis_index("row")
    col = lax.axis_index("col")
    is_source = row < col
    is_lower = row > col
    works = row >= col
    core = col % 2
    chip = col // 2

    def at(r, c):
        return (r, c)

    barrier = pltpu.get_barrier_semaphore()

    def greet(r, c):
        pl.semaphore_signal(barrier, inc=1, device_id=at(r, c), device_id_type=MESH)

    relays = []
    for j in range(DIRECT, PIECES):
        for cls in range(3):
            flip, mask = PLAN[cls][j]
            k = row ^ (8 * flip)
            r = col ^ mask
            a, b = ((0, 0), (0, 1), (1, 1))[cls]
            valid = (k < r) & (k // 8 == a) & (r // 8 == b)
            relays.append((cls, j, valid, k, r))
    cls_from = row // 8 + col // 8

    for d in range(1, N):
        greet(row, (col + d) % N)
    for d in range(N):
        greet(row ^ 8, (col + d) % N)

    def along(d):
        return row // 8 * 8 + (row + d) % 8

    near = (1, 2, 6, 7)
    far = (3, 4, 5)
    for d in near:
        greet(along(d), col)

    STEPS = 4
    SR = TILE // STEPS

    def loads(i):
        rows = pl.ds(i * SR, SR)
        return [
            pltpu.make_async_copy(h.at[rows], v.at[rows], load_sem.at[i, n])
            for n, (h, v) in enumerate(
                ((less_hbm, less), (great_hbm, great), (wless_hbm, wless), (wgreat_hbm, wgreat))
            )
        ]

    def own_windows():
        out = []
        for j in range(PIECES):
            rows = pl.ds(j * PIECE, PIECE)
            for n, h in enumerate((less_hbm, great_hbm)):
                out.append(
                    pltpu.make_async_copy(
                        h.at[rows, pl.ds(0, WINDOW)], win.at[j, n], win_recv.at[j]
                    )
                )
        return out

    @pl.when(works)
    def _():
        for i in range(STEPS):
            for cp in loads(i):
                cp.start()

        @pl.when(row == col)
        def _():
            for cp in own_windows():
                cp.start()

    pl.semaphore_wait(barrier, 2 * N - 1 + len(near))

    def first_sends(j, part):
        f = pick(cls_from, [PLAN[c][j][0] for c in range(3)])
        m = pick(cls_from, [PLAN[c][j][1] for c in range(3)])
        h = (less_hbm, great_hbm)[part]
        src = h.at[pl.ds(j * PIECE, PIECE), pl.ds(0, WINDOW)]
        if j < DIRECT:
            return pltpu.make_async_remote_copy(
                src, win.at[j, part], s1_send.at[j, part], win_recv.at[j],
                device_id=at(col, row), device_id_type=MESH,
            )
        slot = (j - DIRECT) * 3 + cls_from
        return pltpu.make_async_remote_copy(
            src, slots.at[slot, part], s1_send.at[j, part], s1_recv.at[slot],
            device_id=at(row ^ (8 * f), col ^ m), device_id_type=MESH,
        )

    @pl.when(is_source)
    def _():
        for j in range(DIRECT, PIECES):
            for part in range(2):
                first_sends(j, part).start()

    def tell(sem, steps):
        for d in steps:
            pl.semaphore_signal(
                sem, inc=1, device_id=at(along(d), col), device_id_type=MESH
            )

    tell(near_sem, near)
    pl.semaphore_wait(near_sem, len(near))
    tell(far_sem, far)

    @pl.when(works)
    def _():
        B = 16
        for i in range(STEPS):
            for cp in loads(i):
                cp.wait()

            @pl.loop(0, SR // B)
            def _(s):
                base = i * SR + s * B
                rows = pl.ds(pl.multiple_of(base, B), B)
                low = less[rows, :].astype(jnp.float32) * wless[rows, :].astype(jnp.float32)
                high = great[rows, :].astype(jnp.float32) * wgreat[rows, :].astype(jnp.float32)
                less_s[rows, :] = low.astype(jnp.bfloat16)
                later = row * TILE + base + lax.broadcasted_iota(jnp.int32, (B, TILE), 0)
                inner = col * TILE + lax.broadcasted_iota(jnp.int32, (B, TILE), 1)
                ret_s[rows, :] = jnp.where(inner <= later, high - low, 0.0).astype(jnp.bfloat16)

    pl.semaphore_wait(far_sem, len(far))

    @pl.when(is_source)
    def _():
        for j in range(DIRECT):
            for part in range(2):
                first_sends(j, part).start()

    def forward(i):
        cls, j, valid, k, r = relays[i]
        return pltpu.make_async_remote_copy(
            slots.at[i], win.at[j], f_send.at[i], win_recv.at[j],
            device_id=at(r, k), device_id_type=MESH,
        )

    for i, (cls, j, valid, k, r) in enumerate(relays):
        @pl.when(valid)
        def _():
            pltpu.make_async_copy(slots.at[i], slots.at[i], s1_recv.at[i]).wait()
            forward(i).start()

    pal_id = at(row, col ^ 1)
    first = core == 0

    def pal_copy(t):
        return pltpu.make_async_remote_copy(
            psend.at[t], pal.at[t], pal_send.at[t], pal_recv.at[t],
            device_id=pal_id, device_id_type=MESH,
        )

    def q_copy(t, d):
        to = (chip + d) % CHIPS
        return pltpu.make_async_remote_copy(
            qsend.at[t, to], qrecv.at[t, chip], q_send.at[t, d], q_recv.at[t, chip],
            device_id=at(row, to * 2 + core), device_id_type=MESH,
        )

    def e_copy(t, to):
        return pltpu.make_async_remote_copy(
            esend.at[t, to], erecv.at[t, chip], e_send.at[t, to], e_recv.at[t, chip],
            device_id=at(row, to * 2 + core), device_id_type=MESH,
        )

    def y_copy(t):
        return pltpu.make_async_remote_copy(
            ysend.at[t], yrecv.at[t], y_send.at[t], y_recv.at[t],
            device_id=pal_id, device_id_type=MESH,
        )

    MB = 512

    @pl.when(works)
    def _():
        for g in range(GROUPS):
            for j in range(g * PER, (g + 1) * PER):
                pltpu.make_async_copy(win.at[j], win.at[j], win_recv.at[j]).wait()
            pieces = pl.ds(g * PER, PER)
            green = win[pieces, 0].reshape(GROUP, WINDOW)
            great_win = win[pieces, 1].reshape(GROUP, WINDOW).astype(jnp.float32)
            diff = (green.astype(jnp.float32) - great_win).astype(jnp.bfloat16)
            inner = col * TILE + g * GROUP + lax.broadcasted_iota(jnp.int32, (GROUP, WINDOW), 0)
            times = row * TILE + lax.broadcasted_iota(jnp.int32, (GROUP, WINDOW), 1)
            diff = jnp.where(inner <= times, diff, jnp.zeros((), jnp.bfloat16))
            us = pl.ds(g * GROUP, GROUP)

            @pl.loop(0, TILE // MB)
            def _(s):
                start = (s + core + 1) * MB % TILE
                rows = pl.ds(pl.multiple_of(start, MB), MB)
                value = jnp.dot(ret_s[rows, us], green, preferred_element_type=jnp.float32)
                value = value + jnp.dot(less_s[rows, us], diff, preferred_element_type=jnp.float32)
                value = value * SCALE
                if g > 0:
                    value = acc[rows, :] + value
                acc[rows, :] = value
                if g == GROUPS - 1:
                    @pl.when(s == 0)
                    def _():
                        psend[...] = value.astype(jnp.bfloat16).reshape(SUBS, SUB, WINDOW)
                        for t in range(SUBS):
                            pal_copy(t).start()

    @pl.when(is_source)
    def _():
        acc[...] = jnp.zeros_like(acc)
        psend[...] = jnp.zeros_like(psend)
        for t in range(SUBS):
            pal_copy(t).start()

    def sub_rows(half, t):
        return pl.ds(pl.multiple_of(half * HALF + t * SUB, SUB), SUB)

    last = CHIPS - 1

    for t in range(SUBS):
        pal_copy(t).wait_recv()
        both = acc[sub_rows(core, t), :] + pal[t].astype(jnp.float32)
        qsend[t] = both.astype(jnp.bfloat16).reshape(CHIPS, PART, WINDOW)

        @pl.when(chip != last)
        def _():
            for d in range(1, CHIPS):
                q_copy(t, d).start()

        qrecv[t, chip] = qsend[t, chip]

    for t in range(SUBS):
        run = jnp.zeros((PART, WINDOW), jnp.float32)
        for m in range(last):
            @pl.when(chip != m)
            def _():
                pltpu.make_async_copy(qrecv.at[t, m], qrecv.at[t, m], q_recv.at[t, m]).wait()

            run = run + qrecv[t, m].astype(jnp.float32)
            esend[t, m + 1] = run.astype(jnp.bfloat16)

            @pl.when(chip != m + 1)
            def _():
                e_copy(t, m + 1).start()

        esend[t, 0] = jnp.zeros((PART, WINDOW), jnp.bfloat16)
        erecv[t, chip] = esend[t, chip]

    for t in range(SUBS):
        @pl.when(chip == 0)
        def _():
            erecv[t] = jnp.zeros((CHIPS, PART, WINDOW), jnp.bfloat16)

        @pl.when(chip != 0)
        def _():
            for m in range(CHIPS):
                @pl.when(chip != m)
                def _():
                    pltpu.make_async_copy(erecv.at[t, m], erecv.at[t, m], e_recv.at[t, m]).wait()

        earlier = erecv[t].astype(jnp.float32).reshape(SUB, WINDOW)
        own = acc[sub_rows(core, t), :]
        ysend[t] = (earlier + jnp.where(first, own, 0.0)).astype(jnp.bfloat16)
        y_copy(t).start()
        before = jnp.where(first, 0.0, pal[t].astype(jnp.float32))
        out_ref[sub_rows(core, t), :] = earlier + before + own

    for t in range(SUBS):
        y_copy(t).wait_recv()
        rows = sub_rows(1 - core, t)
        out_ref[rows, :] = yrecv[t].astype(jnp.float32) + acc[rows, :]

    @pl.when(is_source)
    def _():
        for j in range(PIECES):
            for part in range(2):
                first_sends(j, part).wait_send()

    for i, (cls, j, valid, k, r) in enumerate(relays):
        @pl.when(valid)
        def _():
            forward(i).wait_send()

    for t in range(SUBS):
        pal_copy(t).wait_send()
        y_copy(t).wait_send()

        @pl.when(chip != last)
        def _():
            for d in range(1, CHIPS):
                q_copy(t, d).wait_send()

        for m in range(1, CHIPS):
            @pl.when(chip != m)
            def _():
                e_copy(t, m).wait_send()


def local(lesser, greater, screened_lesser, screened_greater):
    bf16, f32 = jnp.bfloat16, jnp.float32
    n_slots = 3 * (PIECES - DIRECT)
    dma = pltpu.SemaphoreType.DMA
    return pl.pallas_call(
        kernel,
        out_shape=jax.ShapeDtypeStruct((TILE, WINDOW), f32),
        in_specs=[pl.BlockSpec(memory_space=pl.ANY)] * 4,
        out_specs=pl.BlockSpec(memory_space=pltpu.VMEM),
        scratch_shapes=[pltpu.VMEM((TILE, TILE), bf16)] * 6
        + [
            pltpu.VMEM((PIECES, 2, PIECE, WINDOW), bf16),
            pltpu.VMEM((n_slots, 2, PIECE, WINDOW), bf16),
            pltpu.VMEM((TILE, WINDOW), f32),
            pltpu.VMEM((SUBS, SUB, WINDOW), bf16),
            pltpu.VMEM((SUBS, SUB, WINDOW), bf16),
            pltpu.VMEM((SUBS, CHIPS, PART, WINDOW), bf16),
            pltpu.VMEM((SUBS, CHIPS, PART, WINDOW), bf16),
            pltpu.VMEM((SUBS, CHIPS, PART, WINDOW), bf16),
            pltpu.VMEM((SUBS, CHIPS, PART, WINDOW), bf16),
            pltpu.VMEM((SUBS, SUB, WINDOW), bf16),
            pltpu.VMEM((SUBS, SUB, WINDOW), bf16),
            pltpu.SemaphoreType.REGULAR,
            pltpu.SemaphoreType.REGULAR,
            dma((4, 4)),
            dma((PIECES, 2)),
            dma((n_slots,)),
            dma((n_slots,)),
            dma((PIECES,)),
            dma((SUBS,)),
            dma((SUBS,)),
            dma((SUBS, CHIPS)),
            dma((SUBS, CHIPS)),
            dma((SUBS, CHIPS)),
            dma((SUBS, CHIPS)),
            dma((SUBS,)),
            dma((SUBS,)),
        ],
        compiler_params=pltpu.CompilerParams(
            collective_id=0, has_side_effects=True, vmem_limit_bytes=63 << 20
        ),
        name="collision",
    )(lesser, greater, screened_lesser, screened_greater)


def solution(mesh):
    spec = P("row", "col")
    return jax.shard_map(
        local, mesh=mesh, in_specs=(spec,) * 4, out_specs=spec, check_vma=False
    )
```

```python
import functools

import jax
import jax.numpy as jnp
from jax import lax
from jax.experimental import pallas as pl
from jax.experimental.pallas import tpu as pltpu
from jax.sharding import PartitionSpec as P

WINDOW = 256
TILE = 1024
N = 16
CHIPS = 8
SCALE = 2.0**-7
MESH = pl.DeviceIdType.MESH

PLAN = (
    (
        (0, 0), (0, 2), (0, 4), (0, 6), (1, 2), (0, 14), (0, 3), (0, 5),
        (0, 7), (1, 0), (1, 3), (0, 15), (0, 2), (0, 4), (0, 6), (1, 2),
    ),
    (
        (0, 0), (1, 6), (1, 14), (0, 2), (0, 8), (1, 0), (0, 4), (1, 2),
        (1, 4), (1, 7), (1, 15), (0, 3), (0, 9), (1, 1), (1, 6), (1, 14),
    ),
    (
        (0, 0), (0, 12), (0, 2), (0, 4), (0, 8), (1, 0), (1, 4), (0, 13),
        (1, 2), (1, 6), (0, 3), (0, 5), (0, 9), (1, 1), (1, 5), (0, 12),
    ),
)
PIECES = len(PLAN[0])
DIRECT = sum(way == (0, 0) for way in PLAN[0])
PIECE = TILE // PIECES
GROUPS = 4
GROUP = TILE // GROUPS
PER = PIECES // GROUPS
HALF = TILE // 2
SUBS = 2
SUB = HALF // SUBS
PART = SUB // CHIPS


def pick(cls, values):
    out = jnp.int32(values[2])
    out = jnp.where(cls == 1, jnp.int32(values[1]), out)
    return jnp.where(cls == 0, jnp.int32(values[0]), out)


def kernel(
    less_hbm, great_hbm, wless_hbm, wgreat_hbm, out_ref,
    less, great, wless, wgreat, ret_s, less_s, win, slots, acc,
    psend, pal, qsend, qrecv, esend, erecv, ysend, yrecv,
    near_sem, far_sem, load_sem, s1_send, s1_recv, f_send, win_recv,
    pal_send, pal_recv, q_send, q_recv, e_send, e_recv, y_send, y_recv,
):
    row = lax.axis_index("row")
    col = lax.axis_index("col")
    is_source = row < col
    is_lower = row > col
    works = row >= col
    core = col % 2
    chip = col // 2

    def at(r, c):
        return (r, c)

    barrier = pltpu.get_barrier_semaphore()

    def greet(r, c):
        pl.semaphore_signal(barrier, inc=1, device_id=at(r, c), device_id_type=MESH)

    relays = []
    for j in range(DIRECT, PIECES):
        for cls in range(3):
            flip, mask = PLAN[cls][j]
            k = row ^ (8 * flip)
            r = col ^ mask
            a, b = ((0, 0), (0, 1), (1, 1))[cls]
            valid = (k < r) & (k // 8 == a) & (r // 8 == b)
            relays.append((cls, j, valid, k, r))
    cls_from = row // 8 + col // 8


    def along(d):
        return row // 8 * 8 + (row + d) % 8

    near = (1, 2, 6, 7)
    far = (3, 4, 5)
    for d in near:
        greet(along(d), col)
    for d in range(N):
        greet(row ^ 8, (col + d + 8) % N)
    for d in range(1, N):
        greet(row, (col + d) % N)

    STEPS = 4
    SR = TILE // STEPS

    def loads(i):
        rows = pl.ds(i * SR, SR)
        return [
            pltpu.make_async_copy(h.at[rows], v.at[rows], load_sem.at[i, n])
            for n, (h, v) in enumerate(
                ((less_hbm, less), (great_hbm, great), (wless_hbm, wless), (wgreat_hbm, wgreat))
            )
        ]

    def own_windows():
        out = []
        for j in range(PIECES):
            rows = pl.ds(j * PIECE, PIECE)
            for n, h in enumerate((less_hbm, great_hbm)):
                out.append(
                    pltpu.make_async_copy(
                        h.at[rows, pl.ds(0, WINDOW)], win.at[j, n], win_recv.at[j]
                    )
                )
        return out

    @pl.when(works)
    def _():
        for i in range(STEPS):
            for cp in loads(i):
                cp.start()

        @pl.when(row == col)
        def _():
            for cp in own_windows():
                cp.start()

    pl.semaphore_wait(barrier, 2 * N - 1 + len(near))

    def first_sends(j, part):
        f = pick(cls_from, [PLAN[c][j][0] for c in range(3)])
        m = pick(cls_from, [PLAN[c][j][1] for c in range(3)])
        h = (less_hbm, great_hbm)[part]
        src = h.at[pl.ds(j * PIECE, PIECE), pl.ds(0, WINDOW)]
        if j < DIRECT:
            return pltpu.make_async_remote_copy(
                src, win.at[j, part], s1_send.at[j, part], win_recv.at[j],
                device_id=at(col, row), device_id_type=MESH,
            )
        slot = (j - DIRECT) * 3 + cls_from
        return pltpu.make_async_remote_copy(
            src, slots.at[slot, part], s1_send.at[j, part], s1_recv.at[slot],
            device_id=at(row ^ (8 * f), col ^ m), device_id_type=MESH,
        )

    @pl.when(is_source)
    def _():
        for j in range(DIRECT, PIECES):
            for part in range(2):
                first_sends(j, part).start()

    def tell(sem, steps):
        for d in steps:
            pl.semaphore_signal(
                sem, inc=1, device_id=at(along(d), col), device_id_type=MESH
            )

    tell(near_sem, near)
    pl.semaphore_wait(near_sem, len(near))
    tell(far_sem, far)

    @pl.when(works)
    def _():
        B = 16
        for i in range(STEPS):
            for cp in loads(i):
                cp.wait()

            @pl.loop(0, SR // B)
            def _(s):
                base = i * SR + s * B
                rows = pl.ds(pl.multiple_of(base, B), B)
                low = less[rows, :].astype(jnp.float32) * wless[rows, :].astype(jnp.float32)
                high = great[rows, :].astype(jnp.float32) * wgreat[rows, :].astype(jnp.float32)
                less_s[rows, :] = low.astype(jnp.bfloat16)
                later = row * TILE + base + lax.broadcasted_iota(jnp.int32, (B, TILE), 0)
                inner = col * TILE + lax.broadcasted_iota(jnp.int32, (B, TILE), 1)
                ret_s[rows, :] = jnp.where(inner <= later, high - low, 0.0).astype(jnp.bfloat16)

    pl.semaphore_wait(far_sem, len(far))

    @pl.when(is_source)
    def _():
        for j in range(DIRECT):
            for part in range(2):
                first_sends(j, part).start()

    def forward(i):
        cls, j, valid, k, r = relays[i]
        return pltpu.make_async_remote_copy(
            slots.at[i], win.at[j], f_send.at[i], win_recv.at[j],
            device_id=at(r, k), device_id_type=MESH,
        )

    for i, (cls, j, valid, k, r) in enumerate(relays):
        @pl.when(valid)
        def _():
            pltpu.make_async_copy(slots.at[i], slots.at[i], s1_recv.at[i]).wait()
            forward(i).start()

    pal_id = at(row, col ^ 1)
    first = core == 0

    def pal_copy(t):
        return pltpu.make_async_remote_copy(
            psend.at[t], pal.at[t], pal_send.at[t], pal_recv.at[t],
            device_id=pal_id, device_id_type=MESH,
        )

    def q_copy(t, d):
        to = (chip + d) % CHIPS
        return pltpu.make_async_remote_copy(
            qsend.at[t, to], qrecv.at[t, chip], q_send.at[t, d], q_recv.at[t, chip],
            device_id=at(row, to * 2 + core), device_id_type=MESH,
        )

    def e_copy(t, to):
        return pltpu.make_async_remote_copy(
            esend.at[t, to], erecv.at[t, chip], e_send.at[t, to], e_recv.at[t, chip],
            device_id=at(row, to * 2 + core), device_id_type=MESH,
        )

    def y_copy(t):
        return pltpu.make_async_remote_copy(
            ysend.at[t], yrecv.at[t], y_send.at[t], y_recv.at[t],
            device_id=pal_id, device_id_type=MESH,
        )

    MB = 512

    @pl.when(works)
    def _():
        for g in range(GROUPS):
            for j in range(g * PER, (g + 1) * PER):
                pltpu.make_async_copy(win.at[j], win.at[j], win_recv.at[j]).wait()
            pieces = pl.ds(g * PER, PER)
            green = win[pieces, 0].reshape(GROUP, WINDOW)
            great_win = win[pieces, 1].reshape(GROUP, WINDOW).astype(jnp.float32)
            diff = (green.astype(jnp.float32) - great_win).astype(jnp.bfloat16)
            inner = col * TILE + g * GROUP + lax.broadcasted_iota(jnp.int32, (GROUP, WINDOW), 0)
            times = row * TILE + lax.broadcasted_iota(jnp.int32, (GROUP, WINDOW), 1)
            diff = jnp.where(inner <= times, diff, jnp.zeros((), jnp.bfloat16))
            us = pl.ds(g * GROUP, GROUP)

            @pl.loop(0, TILE // MB)
            def _(s):
                start = (s + core + 1) * MB % TILE
                rows = pl.ds(pl.multiple_of(start, MB), MB)
                value = jnp.dot(ret_s[rows, us], green, preferred_element_type=jnp.float32)
                value = value + jnp.dot(less_s[rows, us], diff, preferred_element_type=jnp.float32)
                value = value * SCALE
                if g > 0:
                    value = acc[rows, :] + value
                acc[rows, :] = value
                if g == GROUPS - 1:
                    @pl.when(s == 0)
                    def _():
                        psend[...] = value.astype(jnp.bfloat16).reshape(SUBS, SUB, WINDOW)
                        for t in range(SUBS):
                            pal_copy(t).start()

    @pl.when(is_source)
    def _():
        acc[...] = jnp.zeros_like(acc)
        psend[...] = jnp.zeros_like(psend)
        for t in range(SUBS):
            pal_copy(t).start()

    def sub_rows(half, t):
        return pl.ds(pl.multiple_of(half * HALF + t * SUB, SUB), SUB)

    last = CHIPS - 1

    for t in range(SUBS):
        pal_copy(t).wait_recv()
        both = acc[sub_rows(core, t), :] + pal[t].astype(jnp.float32)
        qsend[t] = both.astype(jnp.bfloat16).reshape(CHIPS, PART, WINDOW)

        @pl.when(chip != last)
        def _():
            for d in range(1, CHIPS):
                q_copy(t, d).start()

        qrecv[t, chip] = qsend[t, chip]

    for t in range(SUBS):
        run = jnp.zeros((PART, WINDOW), jnp.float32)
        for m in range(last):
            @pl.when(chip != m)
            def _():
                pltpu.make_async_copy(qrecv.at[t, m], qrecv.at[t, m], q_recv.at[t, m]).wait()

            run = run + qrecv[t, m].astype(jnp.float32)
            esend[t, m + 1] = run.astype(jnp.bfloat16)

            @pl.when(chip != m + 1)
            def _():
                e_copy(t, m + 1).start()

        esend[t, 0] = jnp.zeros((PART, WINDOW), jnp.bfloat16)
        erecv[t, chip] = esend[t, chip]

    for t in range(SUBS):
        @pl.when(chip == 0)
        def _():
            erecv[t] = jnp.zeros((CHIPS, PART, WINDOW), jnp.bfloat16)

        @pl.when(chip != 0)
        def _():
            for m in range(CHIPS):
                @pl.when(chip != m)
                def _():
                    pltpu.make_async_copy(erecv.at[t, m], erecv.at[t, m], e_recv.at[t, m]).wait()

        earlier = erecv[t].astype(jnp.float32).reshape(SUB, WINDOW)
        own = acc[sub_rows(core, t), :]
        ysend[t] = (earlier + jnp.where(first, own, 0.0)).astype(jnp.bfloat16)
        y_copy(t).start()
        before = jnp.where(first, 0.0, pal[t].astype(jnp.float32))
        out_ref[sub_rows(core, t), :] = earlier + before + own

    for t in range(SUBS):
        y_copy(t).wait_recv()
        rows = sub_rows(1 - core, t)
        out_ref[rows, :] = yrecv[t].astype(jnp.float32) + acc[rows, :]

    @pl.when(is_source)
    def _():
        for j in range(PIECES):
            for part in range(2):
                first_sends(j, part).wait_send()

    for i, (cls, j, valid, k, r) in enumerate(relays):
        @pl.when(valid)
        def _():
            forward(i).wait_send()

    for t in range(SUBS):
        pal_copy(t).wait_send()
        y_copy(t).wait_send()

        @pl.when(chip != last)
        def _():
            for d in range(1, CHIPS):
                q_copy(t, d).wait_send()

        for m in range(1, CHIPS):
            @pl.when(chip != m)
            def _():
                e_copy(t, m).wait_send()


def local(lesser, greater, screened_lesser, screened_greater):
    bf16, f32 = jnp.bfloat16, jnp.float32
    n_slots = 3 * (PIECES - DIRECT)
    dma = pltpu.SemaphoreType.DMA
    return pl.pallas_call(
        kernel,
        out_shape=jax.ShapeDtypeStruct((TILE, WINDOW), f32),
        in_specs=[pl.BlockSpec(memory_space=pl.ANY)] * 4,
        out_specs=pl.BlockSpec(memory_space=pltpu.VMEM),
        scratch_shapes=[pltpu.VMEM((TILE, TILE), bf16)] * 6
        + [
            pltpu.VMEM((PIECES, 2, PIECE, WINDOW), bf16),
            pltpu.VMEM((n_slots, 2, PIECE, WINDOW), bf16),
            pltpu.VMEM((TILE, WINDOW), f32),
            pltpu.VMEM((SUBS, SUB, WINDOW), bf16),
            pltpu.VMEM((SUBS, SUB, WINDOW), bf16),
            pltpu.VMEM((SUBS, CHIPS, PART, WINDOW), bf16),
            pltpu.VMEM((SUBS, CHIPS, PART, WINDOW), bf16),
            pltpu.VMEM((SUBS, CHIPS, PART, WINDOW), bf16),
            pltpu.VMEM((SUBS, CHIPS, PART, WINDOW), bf16),
            pltpu.VMEM((SUBS, SUB, WINDOW), bf16),
            pltpu.VMEM((SUBS, SUB, WINDOW), bf16),
            pltpu.SemaphoreType.REGULAR,
            pltpu.SemaphoreType.REGULAR,
            dma((4, 4)),
            dma((PIECES, 2)),
            dma((n_slots,)),
            dma((n_slots,)),
            dma((PIECES,)),
            dma((SUBS,)),
            dma((SUBS,)),
            dma((SUBS, CHIPS)),
            dma((SUBS, CHIPS)),
            dma((SUBS, CHIPS)),
            dma((SUBS, CHIPS)),
            dma((SUBS,)),
            dma((SUBS,)),
        ],
        compiler_params=pltpu.CompilerParams(
            collective_id=0, has_side_effects=True, vmem_limit_bytes=65575000
        ),
        name="collision",
    )(lesser, greater, screened_lesser, screened_greater)


def solution(mesh):
    spec = P("row", "col")
    return jax.shard_map(
        local, mesh=mesh, in_specs=(spec,) * 4, out_specs=spec, check_vma=False
    )
```
